32 devices in a mesh: row: 8 (over z, y), col: 4 (over x, core).
Axes of the slice: x: 2, y: 2, z: 4, core: 2. Of those that a mesh axis runs over, the one named last changes fastest.
Arguments:
- start_block: float32 [64, 16, 128], P(('row', 'col')), may hold values from -6 to 6
- blocks: float32 [8, 4, 58, 128, 128], P('row', 'col'), as said below
- slot_row: int32 [8, 4, 58], P('row', 'col'), may hold values from 0 to 7, as said below
- slot_col: int32 [8, 4, 58], P('row', 'col'), may hold values from 0 to 15, as said below
- counts: int32 [8, 4], P('row', 'col'), may hold values from 34 to 58, as said below
Outputs:
- alphas: float32 [2, 16, 16], replicated
- betas: float32 [2, 16, 16], replicated
- next_block: float32 [64, 16, 128], P(('row', 'col'))
The draws below stay inside these ranges and needn't reach their ends.
Inputs may be any that keep to these rules, and one draw needn't show every extreme that they name: `blocks`: over all cells the live slots list each nonzero block of a symmetric matrix exactly once: block (J, I) is listed exactly when (I, J) is, holding its transpose. Slots at or past a cell's count hold finite values that are no part of H. `counts`: live slots of a cell come first; in every draw some cell has all 58 slots live. `slot_row`: for live slots, the block row within the cell's row group of 8 block rows. `slot_col`: for live slots, the position within the cell's column group of 16 block columns, as in the first step.
All inputs are finite; a program needn't handle non-finite values.
Results may differ from the reference program's by a relative error of at most 0.0003.
Values sent between devices are 32-bit elements; how exact they have to be, the bound alone decides.
A program may use at most 64 MiB of HBM per device.

```python
import jax
import jax.numpy as jnp
from jax import lax

ORB = 128
NVEC = 16
PIECE = 2
ITERS = 2
GR = 8
GC = 4
NB = 64
HALF = 8
EXTRA = 24
CAP = 58


def block_pattern(key):
    base_key = jax.random.fold_in(key, 1717)
    group_rows = GC * PIECE
    group_cols = GR * PIECE
    offsets = jax.random.permutation(jax.random.fold_in(base_key, 1), NB // 2 - 1)[:HALF].astype(jnp.int32) + 1
    deltas = jnp.concatenate([jnp.zeros((1,), jnp.int32), offsets, -offsets])
    cell_rows = jnp.arange(GR, dtype=jnp.int32)
    cell_cols = jnp.arange(GC, dtype=jnp.int32)
    local_rows = jnp.arange(group_rows, dtype=jnp.int32)
    first_rows = cell_rows[:, None, None, None] * group_rows + local_rows[None, None, None, :]
    first_cols = jnp.mod(first_rows + deltas[None, None, :, None], NB)
    owners = first_cols // PIECE % GC
    matched = owners == cell_cols[None, :, None, None]
    picked = jnp.argsort(jnp.where(matched, 0, 1), axis=-1, stable=True)[..., :PIECE].astype(jnp.int32)
    base_row = cell_rows[:, None, None, None] * group_rows + picked
    base_col = jnp.mod(base_row + deltas[None, None, :, None], NB)
    base_row = base_row.reshape(GR, GC, -1)
    base_col = base_col.reshape(GR, GC, -1)
    hot_row = jax.random.randint(jax.random.fold_in(base_key, 2), (), 0, GR).astype(jnp.int32)
    hot_col = jax.random.randint(jax.random.fold_in(base_key, 3), (), 0, GC).astype(jnp.int32)
    outside = (GR - 1) * PIECE
    candidate = jnp.arange(group_rows * outside, dtype=jnp.int32)
    local_a = candidate // outside
    local_b = candidate % outside
    position = local_b + PIECE * (local_b // PIECE >= hot_row).astype(jnp.int32)
    extra_row = hot_row * group_rows + local_a
    extra_col = (position // PIECE * GC + hot_col) * PIECE + position % PIECE
    clashes = jnp.any(jnp.mod(extra_col - extra_row, NB)[:, None] == jnp.mod(deltas, NB)[None, :], axis=1)
    ranking = jax.random.permutation(jax.random.fold_in(base_key, 4), candidate.shape[0]).astype(jnp.int32)
    priority = ranking + clashes.astype(jnp.int32) * candidate.shape[0]
    chosen = jnp.argsort(priority, stable=True)[:EXTRA]
    extra_row = extra_row[chosen]
    extra_col = extra_col[chosen]
    mirror_row = extra_col // group_rows
    mirror_col = extra_row // PIECE % GC
    is_hot = (cell_rows[:, None, None] == hot_row) & (cell_cols[None, :, None] == hot_col)
    is_mirror = (mirror_row[None, None, :] == cell_rows[:, None, None]) & (mirror_col[None, None, :] == cell_cols[None, :, None])
    taken_slots = is_hot | is_mirror
    side_row = jnp.where(is_hot, extra_row[None, None, :], extra_col[None, None, :])
    side_col = jnp.where(is_hot, extra_col[None, None, :], extra_row[None, None, :])
    packing = jnp.argsort(jnp.where(taken_slots, 0, 1), axis=-1, stable=True)
    side_row = jnp.take_along_axis(side_row, packing, axis=-1)
    side_col = jnp.take_along_axis(side_col, packing, axis=-1)
    taken_slots = jnp.take_along_axis(taken_slots, packing, axis=-1)
    glob_row = jnp.concatenate([base_row, side_row], axis=-1)
    glob_col = jnp.concatenate([base_col, side_col], axis=-1)
    active = jnp.concatenate([jnp.ones(base_row.shape, bool), taken_slots], axis=-1)
    slot_ids = jnp.arange(CAP, dtype=jnp.int32)
    mixing = jax.random.randint(jax.random.fold_in(base_key, 5), (GR, GC, CAP), 0, 1 << 14).astype(jnp.int32) * CAP + slot_ids
    order_key = jnp.where(active, mixing, (1 << 14) * CAP + slot_ids)
    shuffle = jnp.argsort(order_key, axis=-1, stable=True)
    glob_row = jnp.take_along_axis(glob_row, shuffle, axis=-1)
    glob_col = jnp.take_along_axis(glob_col, shuffle, axis=-1)
    active = jnp.take_along_axis(active, shuffle, axis=-1)
    counts = jnp.sum(active.astype(jnp.int32), axis=-1).astype(jnp.int32)
    junk_rows = jax.random.randint(jax.random.fold_in(base_key, 6), (GR, GC, CAP), 0, group_rows).astype(jnp.int32)
    junk_cols = jax.random.randint(jax.random.fold_in(base_key, 7), (GR, GC, CAP), 0, group_cols).astype(jnp.int32)
    slot_row = jnp.where(active, glob_row - cell_rows[:, None, None] * group_rows, junk_rows)
    pieces_of = glob_col // PIECE
    slot_col = jnp.where(active, pieces_of // GC * PIECE + glob_col % PIECE, junk_cols)
    return (slot_row, slot_col, counts, glob_row, glob_col, active)


def draw_slot_row(key, part):
    return block_pattern(key)[0]


def draw_slot_col(key, part):
    return block_pattern(key)[1]


def draw_counts(key, part):
    return block_pattern(key)[2]


def draw_blocks(key, part):
    slot_row, slot_col, counts, glob_row, glob_col, active = block_pattern(key)
    value_key = jax.random.fold_in(key, 2929)
    sigma = (ORB * (2 * HALF + 1)) ** (-0.5)
    slot_ids = jnp.arange(CAP, dtype=jnp.int32)[None, None, :]
    cell_ids = jnp.arange(GR, dtype=jnp.int32)[:, None, None] * GC + jnp.arange(GC, dtype=jnp.int32)[None, :, None]
    lower_id = jnp.where(active, jnp.minimum(glob_row, glob_col), NB + slot_ids)
    upper_id = jnp.where(active, jnp.maximum(glob_row, glob_col), cell_ids + 0 * slot_ids)
    flipped = glob_row > glob_col
    diagonal = active & (glob_row == glob_col)

    def one_tile(lower_one, upper_one, flip_one, diag_one):
        tile_key = jax.random.fold_in(jax.random.fold_in(value_key, lower_one), upper_one)
        raw = jax.random.normal(tile_key, (ORB, ORB), jnp.float32)
        onsite = jax.random.uniform(jax.random.fold_in(tile_key, 5), (ORB,), jnp.float32, -1.0, 3.0)
        drawn = jnp.where(flip_one, raw.T, raw) * sigma
        mirrored = (raw + raw.T) * (sigma * 0.70710678) + jnp.diag(onsite)
        return jnp.where(diag_one, mirrored, drawn)

    def one_cell(item):
        return jax.vmap(one_tile)(item[0], item[1], item[2], item[3])
    cells = GR * GC
    tiles_all = lax.map(one_cell, (lower_id.reshape(cells, CAP), upper_id.reshape(cells, CAP), flipped.reshape(cells, CAP), diagonal.reshape(cells, CAP)))
    return tiles_all.reshape(GR, GC, CAP, ORB, ORB)


def level_of(stream_key, shape, split, low, largest):
    level, own = 1.0, jax.random.fold_in(stream_key, 6)
    for dim, parts in split:
        steps = jnp.exp(jax.random.uniform(jax.random.fold_in(own, dim), (parts,), jnp.float32, low / len(split), largest / len(split)))
        level = level * jnp.repeat(steps, shape[dim] // parts).reshape([-1 if axis == dim else 1 for axis in range(len(shape))])
    return level


def gaussian(own_key, dims, width, reach, shards=(), held_as=jnp.bfloat16):
    factor_of = level_of(own_key, dims, shards, -0.22, 0.18) if shards else 1.0
    entries = jax.random.normal(own_key, dims, jnp.float32) * width * factor_of
    return jnp.minimum(jnp.maximum(entries, -reach), reach).astype(held_as)


def setup_inputs(seed: int = 0) -> dict:
    seeds = jax.random.split(jax.random.key(seed), 6)
    start_block = gaussian(seeds[0], (NB, NVEC, ORB), 1.0, 6.0, ((0, 32),), jnp.float32)
    blocks = draw_blocks(jax.random.fold_in(seeds[5], 71), 0)
    slot_row = draw_slot_row(jax.random.fold_in(seeds[5], 71), 0)
    slot_col = draw_slot_col(jax.random.fold_in(seeds[5], 71), 0)
    counts = draw_counts(jax.random.fold_in(seeds[5], 71), 0)
    return dict(start_block=start_block, blocks=blocks, slot_row=slot_row, slot_col=slot_col, counts=counts)


def mean_gram(left, right):
    return jnp.einsum('bki,bli->kl', left, right, precision=lax.Precision.HIGHEST) / (NB * ORB)

def apply_operator(vectors, blocks, slot_row, slot_col, counts):
    cells = GR * GC
    tiles_all = blocks.reshape(cells, CAP, ORB, ORB)
    rows_all = slot_row.reshape(cells, CAP)
    cols_all = slot_col.reshape(cells, CAP)
    count_all = counts.reshape(cells)
    cell_ids = jnp.arange(cells, dtype=jnp.int32)

    def cell_step(running, item):
        tiles_here, rows_here, cols_here, count_here, cell_id = item
        grid_row = cell_id // GC
        grid_col = cell_id % GC
        active = jnp.arange(CAP, dtype=jnp.int32) < count_here
        global_row = (grid_row * GC * PIECE + rows_here).astype(jnp.int32)
        global_col = ((cols_here // PIECE * GC + grid_col) * PIECE + cols_here % PIECE).astype(jnp.int32)
        picked = vectors[global_col]
        product = jnp.einsum('sij,skj->ski', tiles_here, picked, precision=lax.Precision.HIGHEST)
        product = jnp.where(active[:, None, None], product, jnp.zeros_like(product))
        return (running.at[global_row].add(product), None)
    running = jnp.zeros(vectors.shape, jnp.float32)
    running, _ = lax.scan(cell_step, running, (tiles_all, rows_all, cols_all, count_all, cell_ids))
    return running

def reference(start_block, blocks, slot_row, slot_col, counts):
    identity = jnp.eye(NVEC, dtype=jnp.float32)
    factor = jnp.linalg.cholesky(mean_gram(start_block, start_block))
    inverse = jax.scipy.linalg.solve_triangular(factor, identity, lower=True)
    vectors = jnp.einsum('kl,bli->bki', inverse, start_block, precision=lax.Precision.HIGHEST)
    previous = jnp.zeros(vectors.shape, jnp.float32)
    beta_prev = jnp.zeros((NVEC, NVEC), jnp.float32)
    alpha_list = []
    beta_list = []
    for iteration in range(ITERS):
        image_block = apply_operator(vectors, blocks, slot_row, slot_col, counts)
        alpha_block = mean_gram(vectors, image_block)
        residual = image_block - jnp.einsum('lk,bli->bki', alpha_block, vectors, precision=lax.Precision.HIGHEST)
        residual = residual - jnp.einsum('kl,bli->bki', beta_prev, previous, precision=lax.Precision.HIGHEST)
        factor = jnp.linalg.cholesky(mean_gram(residual, residual))
        beta_block = factor.T
        inverse = jax.scipy.linalg.solve_triangular(factor, identity, lower=True)
        previous = vectors
        vectors = jnp.einsum('kl,bli->bki', inverse, residual, precision=lax.Precision.HIGHEST)
        beta_prev = beta_block
        alpha_list.append(alpha_block)
        beta_list.append(beta_block)
    return (jnp.stack(alpha_list), jnp.stack(beta_list), vectors)
```

```python
import functools

import jax
import jax.numpy as jnp
from jax import lax
from jax.experimental import pallas as pl
from jax.experimental.pallas import tpu as pltpu
from jax.sharding import PartitionSpec as P

HIGHEST = lax.Precision.HIGHEST
F32 = jnp.float32
BF16 = jnp.bfloat16
NN = (((1,), (0,)), ((), ()))
NT = (((1,), (1,)), ((), ()))
TN = (((0,), (0,)), ((), ()))


def dot(left, right, dims=NN):
    return lax.dot_general(left, right, dims, precision=HIGHEST, preferred_element_type=F32)


def factor(gram):
    n = gram.shape[0]
    rows = lax.broadcasted_iota(jnp.int32, (n, n), 0)
    cols = lax.broadcasted_iota(jnp.int32, (n, n), 1)
    work = jnp.concatenate([gram, (rows == cols).astype(F32)], axis=1)
    index = lax.broadcasted_iota(jnp.int32, (n, 2 * n), 0)
    for j in range(n - 1):
        ratio = work[j : j + 1, :] / work[j : j + 1, j : j + 1]
        work = work - jnp.where(index > j, work[:, j : j + 1], 0.0) * ratio
    upper = work[:, :n]
    pivots = jnp.sum(jnp.where(rows == cols, upper, 0.0), axis=1, keepdims=True)
    scale = 1.0 / jnp.sqrt(pivots)
    return jnp.where(rows <= cols, upper, 0.0) * scale, work[:, n:] * scale


def pack(gram):
    quarter = gram.shape[0] // 4
    return jnp.concatenate([gram[i * quarter : (i + 1) * quarter] for i in range(4)], axis=1)


def unpack(packed):
    width = packed.shape[1] // 4
    return jnp.concatenate([packed[:, i * width : (i + 1) * width] for i in range(4)], axis=0)


def kernel(
    nr, nc, group, total,
    rows_ref, cols_ref, counts_ref, start_ref, blocks_ref,
    alphas_ref, betas_ref, next_ref,
    tiles, weights, expanded, gat, xhi, xlo, part, scat, ybuf, gsend, grow, gcol_send, gcol,
    load_sem, row_send, row_recv, col_send, col_recv, gr_send, gr_recv, gc_send, gc_recv,
):
    me_r = lax.axis_index("row")
    me_c = lax.axis_index("col")
    capacity = tiles.shape[0]
    piece, k, orb = start_ref.shape
    local_rows = nc * piece
    count = counts_ref[0]

    load = pltpu.make_async_copy(blocks_ref, tiles, load_sem)
    load.start()

    def row_peer(d):
        return (lax.rem(me_r + d, nr), me_c)

    def col_peer(d):
        return (me_r, lax.rem(me_c + d, nc))

    barrier = pltpu.get_barrier_semaphore()
    for d in range(1, nr):
        pl.semaphore_signal(barrier, inc=1, device_id=row_peer(d), device_id_type=pl.DeviceIdType.MESH)
    for d in range(1, nc):
        pl.semaphore_signal(barrier, inc=1, device_id=col_peer(d), device_id_type=pl.DeviceIdType.MESH)
    pl.semaphore_wait(barrier, nr + nc - 2)

    def spread_row(src, dst, send, recv, step):
        copies = []
        for d in range(1, nr):
            copy = pltpu.make_async_remote_copy(
                src_ref=src, dst_ref=dst.at[me_r],
                send_sem=send.at[step, d], recv_sem=recv.at[step, d],
                device_id=row_peer(d), device_id_type=pl.DeviceIdType.MESH,
            )
            copy.start()
            copies.append(copy)
        return copies

    def spread_col(src, dst, send, recv, step, scatter):
        copies = []
        for d in range(1, nc):
            peer = lax.rem(me_c + d, nc)
            copy = pltpu.make_async_remote_copy(
                src_ref=src.at[peer] if scatter else src, dst_ref=dst.at[me_c],
                send_sem=send.at[step, d], recv_sem=recv.at[step, d],
                device_id=(me_r, peer), device_id_type=pl.DeviceIdType.MESH,
            )
            copy.start()
            copies.append(copy)
        return copies

    def received(copies):
        for copy in copies:
            copy.wait_recv()

    def cat(value):
        return jnp.concatenate([value[p] for p in range(piece)], axis=1)

    pending = []
    first = spread_row(start_ref, gat.at[0], row_send, row_recv, 0)
    pending += first
    gat[0, pl.ds(me_r, 1)] = start_ref[...][None]

    load.wait()

    def split_tile(s, carry):
        tile = lax.select(jnp.broadcast_to(s < count, (orb, orb)), tiles[s], jnp.zeros((orb, orb), F32))
        high = tile.astype(BF16)
        weights[s, :orb] = high
        weights[s, orb:] = (tile - high.astype(F32)).astype(BF16)
        return carry

    lax.fori_loop(0, capacity, split_tile, 0, unroll=2)

    half = local_rows * k

    def operate(step):
        def split_vectors(q, carry):
            for p in range(piece):
                value = gat[step, q, p]
                high = value.astype(BF16)
                xhi[q * piece + p] = high
                xlo[q * piece + p] = (value - high.astype(F32)).astype(BF16)
            return carry

        lax.fori_loop(0, nr, split_vectors, 0, unroll=nr <= 8)

        def chunk(base):
            for t in range(group):
                s = base + t
                col = jnp.clip(lax.select(s < count, cols_ref[s], 0), 0, nr * piece - 1)
                row = rows_ref[s]
                high, low = xhi[col], xlo[col]
                zero = jnp.zeros_like(high)
                for r in range(local_rows):
                    hit = row == r
                    expanded[r * k : (r + 1) * k, t * orb : (t + 1) * orb] = lax.select(hit, high, zero)
                    expanded[half + r * k : half + (r + 1) * k, t * orb : (t + 1) * orb] = lax.select(hit, low, zero)
            flat = jnp.concatenate([weights[base + t] for t in range(group)], axis=1)
            return lax.dot_general(expanded[...], flat, NT, preferred_element_type=F32)

        if capacity == group:
            acc = chunk(0)
        else:
            acc = lax.fori_loop(
                0, capacity // group, lambda g, a: a + chunk(g * group),
                jnp.zeros((2 * half, 2 * orb), F32),
            )
        out = acc[:half, :orb] + acc[:half, orb:] + acc[half:, :orb]
        for r in range(local_rows):
            part[step, r // piece, r % piece] = out[r * k : (r + 1) * k]
        return spread_col(part.at[step], scat.at[step], col_send, col_recv, step, True)

    def reduced(step, copies):
        received(copies)
        own = part[step, me_c]
        for d in range(1, nc):
            own = own + scat[step, lax.rem(me_c + d, nc)]
        return own

    def mean_start(step, gram):
        gsend[step] = pack(gram) * (1.0 / total)
        return spread_row(gsend.at[step], grow.at[step], gr_send, gr_recv, step)

    def mean_middle(step, copies):
        received(copies)
        grow[step, pl.ds(me_r, 1)] = gsend[step][None]
        value = grow[step, 0]
        for r in range(1, nr):
            value = value + grow[step, r]
        gcol_send[step] = value
        return spread_col(gcol_send.at[step], gcol.at[step], gc_send, gc_recv, step, False)

    def mean_end(step, copies):
        received(copies)
        gcol[step, pl.ds(me_c, 1)] = gcol_send[step][None]
        value = gcol[step, 0]
        for c in range(1, nc):
            value = value + gcol[step, c]
        return unpack(value)

    received(first)
    scatter0 = operate(0)
    pending += scatter0
    y_raw = reduced(0, scatter0)
    ybuf[...] = y_raw
    gat[1, pl.ds(me_r, 1)] = y_raw[None]
    second = spread_row(ybuf, gat.at[1], row_send, row_recv, 1)
    pending += second
    s_cat = cat(start_ref)
    y_cat = cat(y_raw)
    both = jnp.concatenate([s_cat, y_cat], axis=0)
    mean0 = mean_start(0, dot(both, both, NT))
    pending += mean0
    received(second)
    middle0 = mean_middle(0, mean0)
    pending += middle0
    scatter1 = operate(1)
    pending += scatter1
    gram = mean_end(0, middle0)
    ss, sy, yy = gram[:k, :k], gram[:k, k:], gram[k:, k:]
    _, inv0 = factor(ss)
    alpha1 = dot(dot(inv0, sy), inv0, NT)
    q1 = dot(dot(inv0, ss), inv0, NT)
    yy1 = dot(dot(inv0, yy), inv0, NT)
    beta1, inv1 = factor(yy1 - dot(alpha1, alpha1, TN) - dot(alpha1, alpha1 - dot(q1, alpha1), TN))
    v1 = dot(inv0, s_cat)
    hv1 = dot(inv0, y_cat)
    v2 = dot(inv1, hv1 - dot(alpha1, v1, TN))
    known = dot(beta1, v1)
    shift = dot(dot(inv1, alpha1, NT), hv1)
    lead = dot(inv1, inv0)
    y2 = dot(lead, cat(reduced(1, scatter1))) - shift
    w2 = y2 - known
    both = jnp.concatenate([v2, w2], axis=0)
    grams = dot(both, jnp.concatenate([both, y2], axis=0), NT)
    top = grams[:k, : 2 * k]
    low = jnp.concatenate([grams[:k, 2 * k :], grams[k:, k : 2 * k]], axis=1)
    mean1 = mean_start(1, jnp.concatenate([top, low], axis=0))
    pending += mean1
    middle1 = mean_middle(1, mean1)
    pending += middle1
    gram = mean_end(1, middle1)
    qq, pw, alpha2, ww = gram[:k, :k], gram[:k, k:], gram[k:, :k], gram[k:, k:]
    rest = pw - dot(qq, alpha2)
    beta2, inv2 = factor(ww - dot(pw, alpha2, TN) - dot(alpha2, rest, TN))
    out = dot(inv2, w2 - dot(alpha2, v2, TN))
    for p in range(piece):
        next_ref[p] = out[:, p * orb : (p + 1) * orb]
    alphas_ref[0] = alpha1
    alphas_ref[1] = alpha2
    betas_ref[0] = beta1
    betas_ref[1] = beta2
    for copy in pending:
        copy.wait_send()


def on_device(nr, nc, start_block, blocks, slot_row, slot_col, counts):
    capacity = blocks.shape[2]
    orb = blocks.shape[3]
    piece, k, _ = start_block.shape
    local_rows = nc * piece
    total = float(piece * nr * nc * orb)
    group = max(g for g in range(1, 65) if capacity % g == 0 and g * local_rows * k <= 64 * 128)
    vmem = pl.BlockSpec(memory_space=pltpu.VMEM)
    smem = pl.BlockSpec(memory_space=pltpu.SMEM)
    dma = pltpu.SemaphoreType.DMA
    width = 4 * 2 * k
    height = 2 * k // 4
    return pl.pallas_call(
        functools.partial(kernel, nr, nc, group, total),
        out_shape=(
            jax.ShapeDtypeStruct((2, k, k), F32),
            jax.ShapeDtypeStruct((2, k, k), F32),
            jax.ShapeDtypeStruct((piece, k, orb), F32),
        ),
        in_specs=[smem, smem, smem, vmem, pl.BlockSpec(memory_space=pl.ANY)],
        out_specs=(vmem, vmem, vmem),
        scratch_shapes=[
            pltpu.VMEM((capacity, orb, orb), F32),
            pltpu.VMEM((capacity, 2 * orb, orb), BF16),
            pltpu.VMEM((2 * local_rows * k, group * orb), BF16),
            pltpu.VMEM((2, nr, piece, k, orb), F32),
            pltpu.VMEM((nr * piece, k, orb), BF16),
            pltpu.VMEM((nr * piece, k, orb), BF16),
            pltpu.VMEM((2, nc, piece, k, orb), F32),
            pltpu.VMEM((2, nc, piece, k, orb), F32),
            pltpu.VMEM((piece, k, orb), F32),
            pltpu.VMEM((2, height, width), F32),
            pltpu.VMEM((2, nr, height, width), F32),
            pltpu.VMEM((2, height, width), F32),
            pltpu.VMEM((2, nc, height, width), F32),
            dma,
            dma((2, nr)), dma((2, nr)),
            dma((2, nc)), dma((2, nc)),
            dma((2, nr)), dma((2, nr)),
            dma((2, nc)), dma((2, nc)),
        ],
        compiler_params=pltpu.CompilerParams(
            collective_id=0, has_side_effects=True, vmem_limit_bytes=60 * 1024 * 1024
        ),
    )(slot_row[0, 0], slot_col[0, 0], counts[0], start_block, blocks[0, 0])


def solution(mesh):
    placed = (
        P(("row", "col"), None, None),
        P("row", "col", None, None, None),
        P("row", "col", None),
        P("row", "col", None),
        P("row", "col"),
    )
    return jax.shard_map(
        functools.partial(on_device, mesh.shape["row"], mesh.shape["col"]),
        mesh=mesh,
        in_specs=placed,
        out_specs=(P(), P(), P(("row", "col"), None, None)),
        check_vma=False,
    )
```

```python
import functools

import jax
import jax.numpy as jnp
from jax import lax
from jax.experimental import pallas as pl
from jax.experimental.pallas import tpu as pltpu
from jax.sharding import PartitionSpec as P

HIGHEST = lax.Precision.HIGHEST
F32 = jnp.float32
BF16 = jnp.bfloat16
NN = (((1,), (0,)), ((), ()))
NT = (((1,), (1,)), ((), ()))
TN = (((0,), (0,)), ((), ()))


def dot(left, right, dims=NN):
    return lax.dot_general(left, right, dims, precision=HIGHEST, preferred_element_type=F32)


def factor(gram):
    n = gram.shape[0]
    rows = lax.broadcasted_iota(jnp.int32, (n, n), 0)
    cols = lax.broadcasted_iota(jnp.int32, (n, n), 1)
    work = jnp.concatenate([gram, (rows == cols).astype(F32)], axis=1)
    index = lax.broadcasted_iota(jnp.int32, (n, 2 * n), 0)
    for j in range(n - 1):
        ratio = work[j : j + 1, :] / work[j : j + 1, j : j + 1]
        work = work - jnp.where(index > j, work[:, j : j + 1], 0.0) * ratio
    upper = work[:, :n]
    pivots = jnp.sum(jnp.where(rows == cols, upper, 0.0), axis=1, keepdims=True)
    scale = 1.0 / jnp.sqrt(pivots)
    return jnp.where(rows <= cols, upper, 0.0) * scale, work[:, n:] * scale


def pack(gram):
    quarter = gram.shape[0] // 4
    return jnp.concatenate([gram[i * quarter : (i + 1) * quarter] for i in range(4)], axis=1)


def unpack(packed):
    width = packed.shape[1] // 4
    return jnp.concatenate([packed[:, i * width : (i + 1) * width] for i in range(4)], axis=0)


def kernel(
    nr, nc, group, total,
    rows_hbm, cols_hbm, counts_hbm, start_ref, blocks_ref,
    packed_ref,
    tiles, weights, expanded, gat, xhi, xlo, part, scat, ybuf, gsend, grow, gcol_send, gcol,
    rows_ref, cols_ref, counts_ref,
    load_sem, row_send, row_recv, col_send, col_recv, gr_send, gr_recv, gc_send, gc_recv,
):
    me_r = lax.axis_index("row")
    me_c = lax.axis_index("col")
    capacity = tiles.shape[0]
    piece, k, orb = start_ref.shape
    local_rows = nc * piece

    loads = [
        pltpu.make_async_copy(start_ref, gat.at[0, me_r], load_sem.at[0]),
        pltpu.make_async_copy(rows_hbm, rows_ref, load_sem.at[1]),
        pltpu.make_async_copy(cols_hbm, cols_ref, load_sem.at[2]),
        pltpu.make_async_copy(counts_hbm, counts_ref, load_sem.at[3]),
        pltpu.make_async_copy(blocks_ref, tiles, load_sem.at[4]),
    ]

    def row_peer(d):
        return (lax.rem(me_r + d, nr), me_c)

    def col_peer(d):
        return (me_r, lax.rem(me_c + d, nc))

    barrier = pltpu.get_barrier_semaphore()
    for d in range(1, nr):
        pl.semaphore_signal(barrier, inc=1, device_id=row_peer(d), device_id_type=pl.DeviceIdType.MESH)
    for d in range(1, nc):
        pl.semaphore_signal(barrier, inc=1, device_id=col_peer(d), device_id_type=pl.DeviceIdType.MESH)
    for load in loads:
        load.start()
    pl.semaphore_wait(barrier, nr + nc - 2)

    def spread_row(src, dst, send, recv, step):
        copies = []
        for d in range(1, nr):
            copy = pltpu.make_async_remote_copy(
                src_ref=src, dst_ref=dst.at[me_r],
                send_sem=send.at[step, d], recv_sem=recv.at[step, d],
                device_id=row_peer(d), device_id_type=pl.DeviceIdType.MESH,
            )
            copy.start()
            copies.append(copy)
        return copies

    def spread_col(src, dst, send, recv, step, scatter):
        copies = []
        for d in range(1, nc):
            peer = lax.rem(me_c + d, nc)
            copy = pltpu.make_async_remote_copy(
                src_ref=src.at[peer] if scatter else src, dst_ref=dst.at[me_c],
                send_sem=send.at[step, d], recv_sem=recv.at[step, d],
                device_id=(me_r, peer), device_id_type=pl.DeviceIdType.MESH,
            )
            copy.start()
            copies.append(copy)
        return copies

    def received(copies):
        for copy in copies:
            copy.wait_recv()

    def cat(value):
        return jnp.concatenate([value[p] for p in range(piece)], axis=1)

    pending = []
    first = spread_row(start_ref, gat.at[0], row_send, row_recv, 0)
    pending += first
    def mean_start(step, gram):
        gsend[step] = pack(gram) * (1.0 / total)
        return spread_row(gsend.at[step], grow.at[step], gr_send, gr_recv, step)

    def mean_middle(step, copies):
        received(copies)
        grow[step, pl.ds(me_r, 1)] = gsend[step][None]
        value = grow[step, 0]
        for r in range(1, nr):
            value = value + grow[step, r]
        gcol_send[step] = value
        return spread_col(gcol_send.at[step], gcol.at[step], gc_send, gc_recv, step, False)

    def mean_end(step, copies):
        received(copies)
        gcol[step, pl.ds(me_c, 1)] = gcol_send[step][None]
        value = gcol[step, 0]
        for c in range(1, nc):
            value = value + gcol[step, c]
        return unpack(value)

    loads[0].wait()
    s_cat = cat(gat[0, me_r])
    ss = dot(s_cat, s_cat, NT)
    ss = jnp.concatenate([ss, ss], axis=1)
    mean_s = mean_start(0, jnp.concatenate([ss, ss], axis=0))
    pending += mean_s
    for load in loads[1:]:
        load.wait()
    count = counts_ref[0, 0]

    def split_tile(s, carry):
        tile = lax.select(jnp.broadcast_to(s < count, (orb, orb)), tiles[s], jnp.zeros((orb, orb), F32))
        high = tile.astype(BF16)
        weights[s, :orb] = high
        weights[s, orb:] = (tile - high.astype(F32)).astype(BF16)
        return carry

    lax.fori_loop(0, capacity, split_tile, 0, unroll=2)

    half = local_rows * k

    def operate(step):
        def split_vectors(q, carry):
            for p in range(piece):
                value = gat[step, q, p]
                high = value.astype(BF16)
                xhi[q * piece + p] = high
                xlo[q * piece + p] = (value - high.astype(F32)).astype(BF16)
            return carry

        lax.fori_loop(0, nr, split_vectors, 0, unroll=nr <= 8)

        def chunk(base):
            for t in range(group):
                s = base + t
                col = jnp.clip(lax.select(s < count, cols_ref[s], 0), 0, nr * piece - 1)
                row = rows_ref[s]
                high, low = xhi[col], xlo[col]
                zero = jnp.zeros_like(high)
                for r in range(local_rows):
                    hit = row == r
                    expanded[r * k : (r + 1) * k, t * orb : (t + 1) * orb] = lax.select(hit, high, zero)
                    expanded[half + r * k : half + (r + 1) * k, t * orb : (t + 1) * orb] = lax.select(hit, low, zero)
            flat = jnp.concatenate([weights[base + t] for t in range(group)], axis=1)
            return lax.dot_general(expanded[...], flat, NT, preferred_element_type=F32)

        if capacity == group:
            acc = chunk(0)
        else:
            acc = lax.fori_loop(
                0, capacity // group, lambda g, a: a + chunk(g * group),
                jnp.zeros((2 * half, 2 * orb), F32),
            )
        out = acc[:half, :orb] + acc[:half, orb:] + acc[half:, :orb]
        for r in range(local_rows):
            part[step, r // piece, r % piece] = out[r * k : (r + 1) * k]
        return spread_col(part.at[step], scat.at[step], col_send, col_recv, step, True)

    def reduced(step, copies):
        received(copies)
        own = part[step, me_c]
        for d in range(1, nc):
            own = own + scat[step, lax.rem(me_c + d, nc)]
        return own

    received(first)
    middle_s = mean_middle(0, mean_s)
    pending += middle_s
    scatter0 = operate(0)
    pending += scatter0
    _, inv0 = factor(mean_end(0, middle_s)[:k, :k])
    v1 = dot(inv0, s_cat)
    y_raw = reduced(0, scatter0)
    ybuf[...] = y_raw
    gat[1, pl.ds(me_r, 1)] = y_raw[None]
    second = spread_row(ybuf, gat.at[1], row_send, row_recv, 1)
    pending += second
    hv1 = dot(inv0, cat(y_raw))
    both = jnp.concatenate([v1, hv1], axis=0)
    mean0 = mean_start(1, dot(both, both, NT))
    pending += mean0
    received(second)
    middle0 = mean_middle(1, mean0)
    pending += middle0
    scatter1 = operate(1)
    pending += scatter1
    gram = mean_end(1, middle0)
    q1, alpha1, yy1 = gram[:k, :k], gram[:k, k:], gram[k:, k:]
    beta1, inv1 = factor(yy1 - dot(alpha1, alpha1, TN) - dot(alpha1, alpha1 - dot(q1, alpha1), TN))
    v2 = dot(inv1, hv1 - dot(alpha1, v1, TN))
    known = dot(beta1, v1)
    shift = dot(dot(inv1, alpha1, NT), hv1)
    lead = dot(inv1, inv0)
    y2 = dot(lead, cat(reduced(1, scatter1))) - shift
    w2 = y2 - known
    both = jnp.concatenate([v2, w2], axis=0)
    grams = dot(both, jnp.concatenate([both, y2], axis=0), NT)
    top = grams[:k, : 2 * k]
    low = jnp.concatenate([grams[:k, 2 * k :], grams[k:, k : 2 * k]], axis=1)
    mean1 = mean_start(2, jnp.concatenate([top, low], axis=0))
    pending += mean1
    middle1 = mean_middle(2, mean1)
    pending += middle1
    gram = mean_end(2, middle1)
    qq, pw, alpha2, ww = gram[:k, :k], gram[:k, k:], gram[k:, :k], gram[k:, k:]
    rest = pw - dot(qq, alpha2)
    beta2, inv2 = factor(ww - dot(pw, alpha2, TN) - dot(alpha2, rest, TN))
    out = dot(inv2, w2 - dot(alpha2, v2, TN))
    for p in range(piece):
        packed_ref[p, :, :orb] = out[:, p * orb : (p + 1) * orb]
    packed_ref[piece, :, : 4 * k] = jnp.concatenate([alpha1, alpha2, beta1, beta2], axis=1)
    for copy in pending:
        copy.wait_send()


def finish(packed_ref, alphas_ref, betas_ref, next_ref):
    piece, k, _ = next_ref.shape
    small = packed_ref[piece]
    for step in range(2):
        alphas_ref[step] = small[:, step * k : (step + 1) * k]
        betas_ref[step] = small[:, (2 + step) * k : (3 + step) * k]
    next_ref[...] = packed_ref[:piece]


def on_device(nr, nc, start_block, blocks, slot_row, slot_col, counts):
    capacity = blocks.shape[2]
    orb = blocks.shape[3]
    piece, k, _ = start_block.shape
    local_rows = nc * piece
    total = float(piece * nr * nc * orb)
    group = max(g for g in range(1, 65) if capacity % g == 0 and g * local_rows * k <= 64 * 128)
    vmem = pl.BlockSpec(memory_space=pltpu.VMEM)
    dma = pltpu.SemaphoreType.DMA
    width = 4 * 2 * k
    height = 2 * k // 4
    packed = pl.pallas_call(
        functools.partial(kernel, nr, nc, group, total),
        out_shape=jax.ShapeDtypeStruct((piece + 1, k, orb), F32),
        in_specs=[pl.BlockSpec(memory_space=pltpu.HBM)] * 5,
        out_specs=vmem,
        scratch_shapes=[
            pltpu.VMEM((capacity, orb, orb), F32),
            pltpu.VMEM((capacity, 2 * orb, orb), BF16),
            pltpu.VMEM((2 * local_rows * k, group * orb), BF16),
            pltpu.VMEM((2, nr, piece, k, orb), F32),
            pltpu.VMEM((nr * piece, k, orb), BF16),
            pltpu.VMEM((nr * piece, k, orb), BF16),
            pltpu.VMEM((2, nc, piece, k, orb), F32),
            pltpu.VMEM((2, nc, piece, k, orb), F32),
            pltpu.VMEM((piece, k, orb), F32),
            pltpu.VMEM((3, height, width), F32),
            pltpu.VMEM((3, nr, height, width), F32),
            pltpu.VMEM((3, height, width), F32),
            pltpu.VMEM((3, nc, height, width), F32),
            pltpu.SMEM((capacity,), jnp.int32),
            pltpu.SMEM((capacity,), jnp.int32),
            pltpu.SMEM((1, 1), jnp.int32),
            dma((5,)),
            dma((2, nr)), dma((2, nr)),
            dma((2, nc)), dma((2, nc)),
            dma((3, nr)), dma((3, nr)),
            dma((3, nc)), dma((3, nc)),
        ],
        compiler_params=pltpu.CompilerParams(
            collective_id=0, has_side_effects=True, vmem_limit_bytes=61 << 20
        ),
    )(slot_row[0, 0], slot_col[0, 0], counts, start_block, blocks[0, 0])
    return pl.pallas_call(
        finish,
        out_shape=(
            jax.ShapeDtypeStruct((2, k, k), F32),
            jax.ShapeDtypeStruct((2, k, k), F32),
            jax.ShapeDtypeStruct((piece, k, orb), F32),
        ),
        in_specs=[vmem],
        out_specs=(vmem, vmem, vmem),
    )(packed)


def solution(mesh):
    placed = (
        P(("row", "col"), None, None),
        P("row", "col", None, None, None),
        P("row", "col", None),
        P("row", "col", None),
        P("row", "col"),
    )
    return jax.shard_map(
        functools.partial(on_device, mesh.shape["row"], mesh.shape["col"]),
        mesh=mesh,
        in_specs=placed,
        out_specs=(P(), P(), P(("row", "col"), None, None)),
        check_vma=False,
    )
```

```python
import functools

import jax
import jax.numpy as jnp
from jax import lax
from jax.experimental import pallas as pl
from jax.experimental.pallas import tpu as pltpu
from jax.sharding import PartitionSpec as P

HIGHEST = lax.Precision.HIGHEST
F32 = jnp.float32
BF16 = jnp.bfloat16
NN = (((1,), (0,)), ((), ()))
NT = (((1,), (1,)), ((), ()))
TN = (((0,), (0,)), ((), ()))


def dot(left, right, dims=NN):
    return lax.dot_general(left, right, dims, precision=HIGHEST, preferred_element_type=F32)


def factor(gram):
    n = gram.shape[0]
    rows = lax.broadcasted_iota(jnp.int32, (n, n), 0)
    cols = lax.broadcasted_iota(jnp.int32, (n, n), 1)
    work = jnp.concatenate([gram, (rows == cols).astype(F32)], axis=1)
    index = lax.broadcasted_iota(jnp.int32, (n, 2 * n), 0)
    for j in range(n - 1):
        ratio = work[j : j + 1, :] / work[j : j + 1, j : j + 1]
        work = work - jnp.where(index > j, work[:, j : j + 1], 0.0) * ratio
    upper = work[:, :n]
    pivots = jnp.sum(jnp.where(rows == cols, upper, 0.0), axis=1, keepdims=True)
    scale = 1.0 / jnp.sqrt(pivots)
    return jnp.where(rows <= cols, upper, 0.0) * scale, work[:, n:] * scale


def pack(gram):
    quarter = gram.shape[0] // 4
    return jnp.concatenate([gram[i * quarter : (i + 1) * quarter] for i in range(4)], axis=1)


def unpack(packed):
    width = packed.shape[1] // 4
    return jnp.concatenate([packed[:, i * width : (i + 1) * width] for i in range(4)], axis=0)


def kernel(
    nr, nc, group, total,
    rows_hbm, cols_hbm, counts_hbm, start_ref, blocks_ref,
    packed_ref,
    tiles, weights, expanded, gat, xhi, xlo, part, scat, ybuf, gsend, grow, gcol_send, gcol,
    rows_ref, cols_ref, counts_ref,
    load_sem, row_send, row_recv, col_send, col_recv, gr_send, gr_recv, gc_send, gc_recv,
):
    me_r = lax.axis_index("row")
    me_c = lax.axis_index("col")
    capacity = tiles.shape[0]
    piece, k, orb = start_ref.shape
    local_rows = nc * piece

    loads = [
        pltpu.make_async_copy(start_ref, gat.at[0, me_r], load_sem.at[0]),
        pltpu.make_async_copy(rows_hbm, rows_ref, load_sem.at[1]),
        pltpu.make_async_copy(cols_hbm, cols_ref, load_sem.at[2]),
        pltpu.make_async_copy(counts_hbm, counts_ref, load_sem.at[3]),
        pltpu.make_async_copy(blocks_ref, tiles, load_sem.at[4]),
    ]

    def row_peer(d):
        return (lax.rem(me_r + d, nr), me_c)

    def col_peer(d):
        return (me_r, lax.rem(me_c + d, nc))

    barrier = pltpu.get_barrier_semaphore()
    for d in range(1, nr):
        pl.semaphore_signal(barrier, inc=1, device_id=row_peer(d), device_id_type=pl.DeviceIdType.MESH)
    for d in range(1, nc):
        pl.semaphore_signal(barrier, inc=1, device_id=col_peer(d), device_id_type=pl.DeviceIdType.MESH)
    for load in loads:
        load.start()
    pl.semaphore_wait(barrier, nr + nc - 2)

    def spread_row(src, dst, send, recv, step):
        copies = []
        for d in range(1, nr):
            copy = pltpu.make_async_remote_copy(
                src_ref=src, dst_ref=dst.at[me_r],
                send_sem=send.at[step, d], recv_sem=recv.at[step, d],
                device_id=row_peer(d), device_id_type=pl.DeviceIdType.MESH,
            )
            copy.start()
            copies.append(copy)
        return copies

    def spread_col(src, dst, send, recv, step, scatter):
        copies = []
        for d in range(1, nc):
            peer = lax.rem(me_c + d, nc)
            copy = pltpu.make_async_remote_copy(
                src_ref=src.at[peer] if scatter else src, dst_ref=dst.at[me_c],
                send_sem=send.at[step, d], recv_sem=recv.at[step, d],
                device_id=(me_r, peer), device_id_type=pl.DeviceIdType.MESH,
            )
            copy.start()
            copies.append(copy)
        return copies

    def received(copies):
        for copy in copies:
            copy.wait_recv()

    def cat(value):
        return jnp.concatenate([value[p] for p in range(piece)], axis=1)

    pending = []
    first = spread_row(start_ref, gat.at[0], row_send, row_recv, 0)
    pending += first
    def mean_start(step, gram):
        gsend[step] = pack(gram) * (1.0 / total)
        return spread_row(gsend.at[step], grow.at[step], gr_send, gr_recv, step)

    def mean_row(step, copies):
        received(copies)
        grow[step, pl.ds(me_r, 1)] = gsend[step][None]
        value = grow[step, 0]
        for r in range(1, nr):
            value = value + grow[step, r]
        return value

    def mean_column(step, value):
        gcol_send[step] = value
        return spread_col(gcol_send.at[step], gcol.at[step], gc_send, gc_recv, step, False)

    def cat_group(step):
        return jnp.concatenate([gat[step, r, p] for r in range(nr) for p in range(piece)], axis=1)

    def mean_end(step, copies):
        received(copies)
        gcol[step, pl.ds(me_c, 1)] = gcol_send[step][None]
        value = gcol[step, 0]
        for c in range(1, nc):
            value = value + gcol[step, c]
        return unpack(value)

    loads[0].wait()
    s_cat = cat(gat[0, me_r])
    for load in loads[1:]:
        load.wait()
    count = counts_ref[0, 0]

    def split_tile(s, carry):
        tile = lax.select(jnp.broadcast_to(s < count, (orb, orb)), tiles[s], jnp.zeros((orb, orb), F32))
        high = tile.astype(BF16)
        weights[s, :orb] = high
        weights[s, orb:] = (tile - high.astype(F32)).astype(BF16)
        return carry

    lax.fori_loop(0, capacity, split_tile, 0, unroll=2)

    half = local_rows * k

    def operate(step):
        def split_vectors(q, carry):
            for p in range(piece):
                value = gat[step, q, p]
                high = value.astype(BF16)
                xhi[q * piece + p] = high
                xlo[q * piece + p] = (value - high.astype(F32)).astype(BF16)
            return carry

        lax.fori_loop(0, nr, split_vectors, 0, unroll=nr <= 8)

        def chunk(base):
            for t in range(group):
                s = base + t
                col = jnp.clip(lax.select(s < count, cols_ref[s], 0), 0, nr * piece - 1)
                row = rows_ref[s]
                high, low = xhi[col], xlo[col]
                zero = jnp.zeros_like(high)
                for r in range(local_rows):
                    hit = row == r
                    expanded[r * k : (r + 1) * k, t * orb : (t + 1) * orb] = lax.select(hit, high, zero)
                    expanded[half + r * k : half + (r + 1) * k, t * orb : (t + 1) * orb] = lax.select(hit, low, zero)
            flat = jnp.concatenate([weights[base + t] for t in range(group)], axis=1)
            return lax.dot_general(expanded[...], flat, NT, preferred_element_type=F32)

        if capacity == group:
            acc = chunk(0)
        else:
            acc = lax.fori_loop(
                0, capacity // group, lambda g, a: a + chunk(g * group),
                jnp.zeros((2 * half, 2 * orb), F32),
            )
        out = acc[:half, :orb] + acc[:half, orb:] + acc[half:, :orb]
        for r in range(local_rows):
            part[step, r // piece, r % piece] = out[r * k : (r + 1) * k]
        return spread_col(part.at[step], scat.at[step], col_send, col_recv, step, True)

    def reduced(step, copies):
        received(copies)
        own = part[step, me_c]
        for d in range(1, nc):
            own = own + scat[step, lax.rem(me_c + d, nc)]
        return own

    received(first)
    s_all = cat_group(0)
    ss = dot(s_all, s_all, NT)
    ss = jnp.concatenate([ss, ss], axis=1)
    middle_s = mean_column(0, pack(jnp.concatenate([ss, ss], axis=0)) * (1.0 / total))
    pending += middle_s
    scatter0 = operate(0)
    pending += scatter0
    _, inv0 = factor(mean_end(0, middle_s)[:k, :k])
    v1 = dot(inv0, s_cat)
    v1_all = dot(inv0, cat_group(0))
    y_raw = reduced(0, scatter0)
    ybuf[...] = y_raw
    gat[1, pl.ds(me_r, 1)] = y_raw[None]
    second = spread_row(ybuf, gat.at[1], row_send, row_recv, 1)
    pending += second
    hv1 = dot(inv0, cat(y_raw))
    received(second)
    both = jnp.concatenate([v1_all, dot(inv0, cat_group(1))], axis=0)
    middle0 = mean_column(1, pack(dot(both, both, NT)) * (1.0 / total))
    pending += middle0
    scatter1 = operate(1)
    pending += scatter1
    gram = mean_end(1, middle0)
    q1, alpha1, yy1 = gram[:k, :k], gram[:k, k:], gram[k:, k:]
    beta1, inv1 = factor(yy1 - dot(alpha1, alpha1, TN) - dot(alpha1, alpha1 - dot(q1, alpha1), TN))
    v2 = dot(inv1, hv1 - dot(alpha1, v1, TN))
    known = dot(beta1, v1)
    shift = dot(dot(inv1, alpha1, NT), hv1)
    lead = dot(inv1, inv0)
    y2 = dot(lead, cat(reduced(1, scatter1))) - shift
    w2 = y2 - known
    both = jnp.concatenate([v2, w2], axis=0)
    grams = dot(both, jnp.concatenate([both, y2], axis=0), NT)
    top = grams[:k, : 2 * k]
    low = jnp.concatenate([grams[:k, 2 * k :], grams[k:, k : 2 * k]], axis=1)
    mean1 = mean_start(0, jnp.concatenate([top, low], axis=0))
    pending += mean1
    middle1 = mean_column(2, mean_row(0, mean1))
    pending += middle1
    gram = mean_end(2, middle1)
    qq, pw, alpha2, ww = gram[:k, :k], gram[:k, k:], gram[k:, :k], gram[k:, k:]
    rest = pw - dot(qq, alpha2)
    beta2, inv2 = factor(ww - dot(pw, alpha2, TN) - dot(alpha2, rest, TN))
    out = dot(inv2, w2 - dot(alpha2, v2, TN))
    for p in range(piece):
        packed_ref[p, :, :orb] = out[:, p * orb : (p + 1) * orb]
    packed_ref[piece, :, : 4 * k] = jnp.concatenate([alpha1, alpha2, beta1, beta2], axis=1)
    for copy in pending:
        copy.wait_send()


def finish(packed_ref, alphas_ref, betas_ref, next_ref):
    piece, k, _ = next_ref.shape
    small = packed_ref[piece]
    for step in range(2):
        alphas_ref[step] = small[:, step * k : (step + 1) * k]
        betas_ref[step] = small[:, (2 + step) * k : (3 + step) * k]
    next_ref[...] = packed_ref[:piece]


def on_device(nr, nc, start_block, blocks, slot_row, slot_col, counts):
    capacity = blocks.shape[2]
    orb = blocks.shape[3]
    piece, k, _ = start_block.shape
    local_rows = nc * piece
    total = float(piece * nr * nc * orb)
    group = max(g for g in range(1, 65) if capacity % g == 0 and g * local_rows * k <= 64 * 128)
    vmem = pl.BlockSpec(memory_space=pltpu.VMEM)
    dma = pltpu.SemaphoreType.DMA
    width = 4 * 2 * k
    height = 2 * k // 4
    packed = pl.pallas_call(
        functools.partial(kernel, nr, nc, group, total),
        out_shape=jax.ShapeDtypeStruct((piece + 1, k, orb), F32),
        in_specs=[pl.BlockSpec(memory_space=pltpu.HBM)] * 5,
        out_specs=vmem,
        scratch_shapes=[
            pltpu.VMEM((capacity, orb, orb), F32),
            pltpu.VMEM((capacity, 2 * orb, orb), BF16),
            pltpu.VMEM((2 * local_rows * k, group * orb), BF16),
            pltpu.VMEM((2, nr, piece, k, orb), F32),
            pltpu.VMEM((nr * piece, k, orb), BF16),
            pltpu.VMEM((nr * piece, k, orb), BF16),
            pltpu.VMEM((2, nc, piece, k, orb), F32),
            pltpu.VMEM((2, nc, piece, k, orb), F32),
            pltpu.VMEM((piece, k, orb), F32),
            pltpu.VMEM((1, height, width), F32),
            pltpu.VMEM((1, nr, height, width), F32),
            pltpu.VMEM((3, height, width), F32),
            pltpu.VMEM((3, nc, height, width), F32),
            pltpu.SMEM((capacity,), jnp.int32),
            pltpu.SMEM((capacity,), jnp.int32),
            pltpu.SMEM((1, 1), jnp.int32),
            dma((5,)),
            dma((2, nr)), dma((2, nr)),
            dma((2, nc)), dma((2, nc)),
            dma((1, nr)), dma((1, nr)),
            dma((3, nc)), dma((3, nc)),
        ],
        compiler_params=pltpu.CompilerParams(
            collective_id=0, has_side_effects=True, vmem_limit_bytes=61 << 20
        ),
    )(slot_row[0, 0], slot_col[0, 0], counts, start_block, blocks[0, 0])
    return pl.pallas_call(
        finish,
        out_shape=(
            jax.ShapeDtypeStruct((2, k, k), F32),
            jax.ShapeDtypeStruct((2, k, k), F32),
            jax.ShapeDtypeStruct((piece, k, orb), F32),
        ),
        in_specs=[vmem],
        out_specs=(vmem, vmem, vmem),
    )(packed)


def solution(mesh):
    placed = (
        P(("row", "col"), None, None),
        P("row", "col", None, None, None),
        P("row", "col", None),
        P("row", "col", None),
        P("row", "col"),
    )
    return jax.shard_map(
        functools.partial(on_device, mesh.shape["row"], mesh.shape["col"]),
        mesh=mesh,
        in_specs=placed,
        out_specs=(P(), P(), P(("row", "col"), None, None)),
        check_vma=False,
    )
```
